512 devices in a mesh: ctx: 128 (over y, z, core), head: 4 (over x).
Axes of the slice: x: 4, y: 8, z: 8, core: 2. Of those that a mesh axis runs over, the one named last changes fastest.
Arguments:
- queries: bfloat16 [16384, 64, 576], P('ctx', 'head'), may hold values from -100 to 100
- latent_cache: bfloat16 [256, 36864], P('ctx'), may hold values from -6 to 6
- selected: int32 [256, 8], P('ctx'), may hold values from -1 to 255, as said below
- value_weight: bfloat16 [64, 512, 128], P('head'), may hold values from -0.25 to 0.25
Outputs:
- attended: bfloat16 [16384, 8192], P(('ctx', 'head'))
The draws below stay inside these ranges and needn't reach their ends.
Inputs may be any that keep to these rules, and one draw needn't show every extreme that they name: `selected`: row b lists distinct key blocks: its first entry is b itself, the others lie below b; where b + 1 < 8 the row holds all of 0 to b and its remaining slots are -1.
All inputs are finite; a program needn't handle non-finite values.
Results may differ from the reference program's by a relative error of at most 0.011.
Values may be sent and summed in bfloat16 or wider, within the bound.
No kernel may reach another device: no remote copies, remote signals or barrier semaphores. Data moves between devices by JAX's collectives and lax.ppermute only.
A program may use at most 64 MiB of HBM per device.

```python
import jax
import jax.numpy as jnp
from jax import lax

DC = 512
DR = 64
DV = 128
HEADS = 64
KBLK = 64
SEL = 8
NBLK = 256
TOKENS = 16384


def build_pair(key):
    cache_key = jax.random.fold_in(key, 11)
    query_key = jax.random.fold_in(key, 12)
    latent_width = DC + DR
    latent_rows = jnp.clip(jax.random.normal(cache_key, (TOKENS, latent_width), jnp.float32), -6.0, 6.0)
    query_vals = jnp.clip(jax.random.normal(query_key, (TOKENS, HEADS, latent_width), jnp.float32), -6.0, 6.0)
    return (latent_rows, query_vals)


def draw_queries(key, part):
    latent_rows, query_vals = build_pair(key)
    return query_vals.astype(jnp.bfloat16)


def draw_latent_cache(key, part):
    latent_rows, query_vals = build_pair(key)
    return latent_rows.reshape(NBLK, KBLK * (DC + DR)).astype(jnp.bfloat16)


def draw_selected(key, part):
    row_index = jnp.arange(NBLK, dtype=jnp.int32)[:, None]
    col_index = jnp.arange(NBLK, dtype=jnp.int32)[None, :]
    jitter = jax.random.randint(jax.random.fold_in(key, 21), (NBLK, NBLK), 0, 2 ** 20, dtype=jnp.int32)
    ranking = jnp.where(col_index < row_index, jitter * NBLK + col_index, -1 - col_index)
    ranked = lax.top_k(ranking, SEL - 1)[0]
    picked = jnp.where(ranked >= 0, ranked % NBLK, -1)
    own_block = jnp.arange(NBLK, dtype=jnp.int32)[:, None]
    return jnp.concatenate([own_block, picked.astype(jnp.int32)], axis=1).astype(jnp.int32)


def block_scale(key, shape, shards, smallest, high):
    loudness = 1.0
    for dim, parts in shards:
        steps = jax.random.uniform(jax.random.fold_in(jax.random.fold_in(key, 6), dim), (parts,), jnp.float32, smallest / len(shards), high / len(shards))
        loudness = loudness * jnp.repeat(jnp.exp(steps), shape[dim] // parts).reshape((-1,) + (1,) * (len(shape) - 1 - dim))
    return loudness


def bell_draw(own_key, shape, width, bound, shards=(), kind=jnp.bfloat16):
    result = jax.random.normal(own_key, shape, jnp.float32) * width
    if len(shards) > 0:
        result = block_scale(own_key, shape, shards, -0.22, 0.18) * result
    return jnp.clip(result, min=-bound, max=bound).astype(kind)


def setup_inputs(seed: int = 0) -> dict:
    key_of = jax.random.split(jax.random.key(seed), 5)
    queries = draw_queries(jax.random.fold_in(key_of[4], 71), 0)
    latent_cache = draw_latent_cache(jax.random.fold_in(key_of[4], 71), 0)
    selected = draw_selected(jax.random.fold_in(key_of[4], 71), 0)
    value_weight = bell_draw(key_of[3], (HEADS, DC, DV), DC ** -0.5, 0.25, ((0, 4),))
    return {"queries": queries, "latent_cache": latent_cache, "selected": selected, "value_weight": value_weight}


def reference(queries, latent_cache, selected, value_weight):
    latent_width = DC + DR
    score_scale = (DV + DR) ** -0.5
    blocked = latent_cache.reshape(NBLK, KBLK, latent_width)
    offsets = jnp.arange(KBLK, dtype=jnp.int32)

    def one_block(block_index):
        chosen_ids = selected[block_index]
        valid_slot = chosen_ids >= 0
        clipped = jnp.maximum(chosen_ids, 0).astype(jnp.int32)
        key_rows = blocked[clipped].reshape(SEL * KBLK, latent_width)
        key_place = (clipped[:, None] * KBLK + offsets[None, :]).reshape(SEL * KBLK)
        key_valid = jnp.repeat(valid_slot, KBLK)
        query_rows = lax.dynamic_slice_in_dim(queries, (block_index * KBLK).astype(jnp.int32), KBLK, 0)
        query_place = block_index * KBLK + offsets
        scores = jnp.einsum("qhc,kc->hqk", query_rows.astype(jnp.float32), key_rows.astype(jnp.float32)) * score_scale
        allowed = key_valid[None, None, :] & (key_place[None, None, :] <= query_place[None, :, None])
        scores = jnp.where(allowed, scores, -1e30)
        largest = jnp.max(scores, axis=2, keepdims=True)
        powered = jnp.exp(scores - largest)
        weights = (powered / jnp.sum(powered, axis=2, keepdims=True)).astype(jnp.bfloat16)
        mixed_latent = jnp.einsum("hqk,kc->qhc", weights.astype(jnp.float32), key_rows[:, :DC].astype(jnp.float32)).astype(jnp.bfloat16)
        expanded = jnp.einsum("qhc,hcv->qhv", mixed_latent.astype(jnp.float32), value_weight.astype(jnp.float32))
        return expanded.astype(jnp.bfloat16).reshape(KBLK, HEADS * DV)

    per_block = lax.map(one_block, jnp.arange(NBLK, dtype=jnp.int32))
    return per_block.reshape(TOKENS, HEADS * DV)
```

```python
import functools

import jax
import jax.numpy as jnp
from jax import lax
from jax.experimental import pallas as pl
from jax.experimental.pallas import tpu as pltpu
from jax.sharding import PartitionSpec as P

DC = 512
DR = 64
DV = 128
KBLK = 64
SEL = 8
WIDTH = DC + DR
ROW = 640
GROUP = 16
HEAD_BLOCK = 4


def attend_kernel(base_ref, q_ref, k_ref, kpos_ref, w_ref, o_ref):
    heads, rows, width = q_ref.shape
    keys = k_ref[...]
    block = pl.program_id(0)
    queries = q_ref[...].reshape(heads * rows, width)
    scores = lax.dot_general(
        queries, keys, (((1,), (1,)), ((), ())), preferred_element_type=jnp.float32
    ) * ((DV + DR) ** -0.5)
    first = (base_ref[0] + block) * KBLK
    query_place = first + lax.broadcasted_iota(jnp.int32, (rows, 1), 0)
    allowed = kpos_ref[0] <= query_place
    scores = scores.reshape(heads, rows, -1)
    scores = jnp.where(allowed[None], scores, -1e30)
    largest = jnp.max(scores, axis=2, keepdims=True)
    powered = jnp.exp(scores - largest)
    weights = (powered / jnp.sum(powered, axis=2, keepdims=True)).astype(jnp.bfloat16)
    mixed = lax.dot_general(
        weights.reshape(heads * rows, -1),
        keys[:, :DC],
        (((1,), (0,)), ((), ())),
        preferred_element_type=jnp.float32,
    ).astype(jnp.bfloat16)
    for head in range(heads):
        expanded = jnp.dot(
            mixed[head * rows : (head + 1) * rows], w_ref[head], preferred_element_type=jnp.float32
        )
        o_ref[:, head * DV : (head + 1) * DV] = expanded.astype(jnp.bfloat16)


def attend(base, queries, keys, key_place, value_weight):
    heads, tokens, width = queries.shape
    blocks = tokens // KBLK
    count = keys.shape[1]
    return pl.pallas_call(
        attend_kernel,
        out_shape=jax.ShapeDtypeStruct((tokens, heads * DV), jnp.bfloat16),
        grid_spec=pltpu.PrefetchScalarGridSpec(
            num_scalar_prefetch=1,
            grid=(blocks, heads // HEAD_BLOCK),
            in_specs=[
                pl.BlockSpec((HEAD_BLOCK, KBLK, width), lambda b, h, base: (h, b, 0)),
                pl.BlockSpec((None, count, width), lambda b, h, base: (b, 0, 0)),
                pl.BlockSpec((1, 1, count), lambda b, h, base: (b, 0, 0)),
                pl.BlockSpec((HEAD_BLOCK, DC, DV), lambda b, h, base: (h, 0, 0)),
            ],
            out_specs=pl.BlockSpec((KBLK, HEAD_BLOCK * DV), lambda b, h, base: (b, h)),
        ),
    )(base, queries, keys, key_place, value_weight)


def per_device(queries, latent_cache, selected, value_weight):
    ctx_size = lax.axis_size("ctx")
    head_size = lax.axis_size("head")
    ctx = lax.axis_index("ctx")
    head = lax.axis_index("head")
    here = selected.shape[0]
    rows = ctx_size // GROUP
    groups = [[row * GROUP + i for i in range(GROUP)] for row in range(rows)]

    cache = latent_cache.reshape(here, KBLK, WIDTH)
    mine = lax.dynamic_slice_in_dim(cache, head * GROUP, GROUP, 1)
    lists = jnp.broadcast_to(selected.astype(jnp.bfloat16)[:, None, :], (here, GROUP, SEL))
    filler = jnp.zeros((here, GROUP, ROW - WIDTH - SEL), jnp.bfloat16)
    mine = jnp.concatenate([mine, lists, filler], axis=2).transpose(1, 0, 2)
    spread = lax.all_to_all(
        jnp.broadcast_to(mine[None], (rows, GROUP, here, ROW)).reshape(ctx_size, here, ROW),
        "ctx", split_axis=0, concat_axis=0, tiled=True,
    )
    table = spread.reshape(ctx_size * here, ROW)
    near = lax.dynamic_slice_in_dim(table, (ctx // GROUP) * GROUP * here, GROUP * here, 0)
    wanted = near[:, WIDTH : WIDTH + SEL].astype(jnp.int32).reshape(-1)
    chosen = wanted[:, None] == jnp.arange(ctx_size * here, dtype=jnp.int32)[None, :]
    picked = jnp.dot(
        chosen.astype(jnp.bfloat16), table[:, :WIDTH], preferred_element_type=jnp.float32
    ).astype(jnp.bfloat16)

    fetched = lax.all_to_all(
        picked.reshape(GROUP, here, SEL, WIDTH), "ctx", split_axis=0, concat_axis=0,
        axis_index_groups=groups, tiled=True,
    )
    shared = lax.all_to_all(
        jnp.broadcast_to(fetched[None], (head_size, GROUP, here, SEL, WIDTH)),
        "head", split_axis=0, concat_axis=0, tiled=True,
    )
    keys = shared.reshape(KBLK, here, SEL, WIDTH).transpose(1, 0, 2, 3).reshape(here, KBLK * SEL, WIDTH)

    offsets = jnp.arange(KBLK, dtype=jnp.int32)
    place = jnp.where(selected[:, None, :] >= 0, selected[:, None, :] * KBLK + offsets[None, :, None], 2**30)
    place = place.reshape(here, 1, KBLK * SEL)
    base = (ctx * here).astype(jnp.int32).reshape(1)
    attended = attend(base, queries.transpose(1, 0, 2), keys, place, value_weight)
    return lax.all_to_all(attended, "head", split_axis=0, concat_axis=1, tiled=True)


def solution(mesh):
    in_specs = (P("ctx", "head", None), P("ctx", None), P("ctx", None), P("head", None, None))
    out_specs = P(("ctx", "head"), None)
    return jax.shard_map(
        per_device, mesh=mesh, in_specs=in_specs, out_specs=out_specs, check_vma=False
    )
```

```python
import jax
import jax.numpy as jnp
from jax import lax
from jax.experimental import pallas as pl
from jax.experimental.pallas import tpu as pltpu
from jax.sharding import PartitionSpec as P

DC = 512
DR = 64
DV = 128
KBLK = 64
SEL = 8
WIDTH = DC + DR
BAND_TOKENS = 2
BAND = BAND_TOKENS * WIDTH
ROW = BAND + 128
Y, Z, CORES = 8, 8, 2
HEAD_BLOCK = 8
FACTOR = (DV + DR) ** -0.5 * 1.4426950408889634


def attend_kernel(base_ref, q_ref, k_ref, place_ref, w_ref, o_ref, keys_ref, bias_ref):
    heads, tokens, width = q_ref.shape
    bands, per_band, _ = k_ref.shape
    blocks = tokens // KBLK
    slots = per_band // blocks
    half = bands * slots

    @pl.when(pl.program_id(0) == 0)
    def _():
        for block in range(blocks):
            picked = slice(block * slots, (block + 1) * slots)
            for token in range(BAND_TOKENS):
                rows = k_ref[:, picked, token * width : (token + 1) * width]
                keys_ref[block, token * half : (token + 1) * half, :] = rows.reshape(half, width)
            first = (base_ref[0] + block) * KBLK
            query_place = first + lax.broadcasted_iota(jnp.int32, (KBLK, 1), 0)
            bias_ref[block] = jnp.where(place_ref[block] <= query_place, 0.0, -1e30)

    for block in range(blocks):
        keys = keys_ref[block]
        here = slice(block * KBLK, (block + 1) * KBLK)
        queries = q_ref[:, here, :].reshape(heads * KBLK, width)
        scores = lax.dot_general(
            queries, keys, (((1,), (1,)), ((), ())), preferred_element_type=jnp.float32
        )
        scores = scores.reshape(heads, KBLK, -1) * FACTOR + bias_ref[block][None]
        powered = jnp.exp2(scores - jnp.max(scores, axis=2, keepdims=True))
        total = jnp.sum(powered, axis=2, keepdims=True)
        mixed = lax.dot_general(
            powered.astype(jnp.bfloat16).reshape(heads * KBLK, -1),
            keys[:, :DC],
            (((1,), (0,)), ((), ())),
            preferred_element_type=jnp.float32,
        ).astype(jnp.bfloat16)
        for head in range(heads):
            expanded = jnp.dot(
                mixed[head * KBLK : (head + 1) * KBLK],
                w_ref[head],
                preferred_element_type=jnp.float32,
            )
            o_ref[here, head * DV : (head + 1) * DV] = (expanded / total[head]).astype(jnp.bfloat16)


def attend(base, queries, keys, place, value_weight):
    heads, tokens, width = queries.shape
    blocks, _, count = place.shape
    return pl.pallas_call(
        attend_kernel,
        out_shape=jax.ShapeDtypeStruct((tokens, heads * DV), jnp.bfloat16),
        grid_spec=pltpu.PrefetchScalarGridSpec(
            num_scalar_prefetch=1,
            grid=(heads // HEAD_BLOCK,),
            in_specs=[
                pl.BlockSpec((HEAD_BLOCK, tokens, width), lambda h, base: (h, 0, 0)),
                pl.BlockSpec(keys.shape, lambda h, base: (0, 0, 0)),
                pl.BlockSpec(place.shape, lambda h, base: (0, 0, 0)),
                pl.BlockSpec((HEAD_BLOCK, DC, DV), lambda h, base: (h, 0, 0)),
            ],
            out_specs=pl.BlockSpec((tokens, HEAD_BLOCK * DV), lambda h, base: (0, h)),
            scratch_shapes=[
                pltpu.VMEM((blocks, count, width), jnp.bfloat16),
                pltpu.VMEM((blocks, KBLK, count), jnp.float32),
            ],
        ),
    )(base, queries, keys, place, value_weight)


def fetch_groups(heads):
    groups = []
    for y in range(Y // 2):
        for z in range(Z // 2):
            groups.append([
                (((2 * y + dy) * Z + 2 * z + dz) * CORES + core) * heads + head
                for head in range(heads)
                for dy in range(2)
                for dz in range(2)
                for core in range(CORES)
            ])
    return groups


def per_device(queries, latent_cache, selected, value_weight):
    ctx_size = lax.axis_size("ctx")
    heads = lax.axis_size("head")
    ctx = lax.axis_index("ctx")
    head = lax.axis_index("head")
    here = selected.shape[0]
    cell = 4 * CORES
    bands = heads * cell

    mine = latent_cache.reshape(here, bands, BAND)
    mine = lax.dynamic_slice_in_dim(mine, head * cell, cell, 1).transpose(1, 0, 2)
    lists = jnp.broadcast_to(selected.astype(jnp.bfloat16), (cell, here, SEL))
    filler = jnp.zeros((cell, here, ROW - BAND - SEL), jnp.bfloat16)
    mine = jnp.concatenate([mine, lists, filler], axis=2).reshape(1, 2, 1, 2, CORES, here, ROW)
    spread = lax.all_to_all(
        jnp.broadcast_to(mine, (Y // 2, 2, Z // 2, 2, CORES, here, ROW)).reshape(ctx_size, here, ROW),
        "ctx",
        split_axis=0,
        concat_axis=0,
        tiled=True,
    )
    table = spread.reshape(ctx_size * here, ROW)

    lists = spread[:, :, BAND : BAND + SEL].reshape(Y // 2, 2, Z // 2, 2, CORES, here, SEL)
    y, z = ctx // (Z * CORES), (ctx // CORES) % Z
    lists = lax.dynamic_slice_in_dim(lists, y // 2, 1, 0)
    lists = lax.dynamic_slice_in_dim(lists, z // 2, 1, 2)
    wanted = lists.astype(jnp.int32).reshape(-1)
    chosen = wanted[:, None] == jnp.arange(ctx_size * here, dtype=jnp.int32)[None, :]
    picked = jnp.dot(
        chosen.astype(jnp.bfloat16), table[:, :BAND], preferred_element_type=jnp.float32
    ).astype(jnp.bfloat16)
    picked = picked.reshape(1, cell, here * SEL, BAND)
    keys = lax.all_to_all(
        jnp.broadcast_to(picked, (heads, cell, here * SEL, BAND)).reshape(bands, here * SEL, BAND),
        ("ctx", "head"),
        split_axis=0,
        concat_axis=0,
        axis_index_groups=fetch_groups(heads),
        tiled=True,
    )

    offsets = (
        jnp.arange(BAND_TOKENS, dtype=jnp.int32)[:, None]
        + BAND_TOKENS * jnp.arange(bands, dtype=jnp.int32)[None, :]
    )
    place = selected[:, None, None, :] * KBLK + offsets[None, :, :, None]
    place = jnp.where(selected[:, None, None, :] >= 0, place, 2**30)
    place = place.reshape(here, 1, SEL * KBLK)
    base = (ctx * here).astype(jnp.int32).reshape(1)
    attended = attend(base, queries.transpose(1, 0, 2), keys, place, value_weight)
    return lax.all_to_all(attended, "head", split_axis=0, concat_axis=1, tiled=True)


def solution(mesh):
    in_specs = (P("ctx", "head", None), P("ctx", None), P("ctx", None), P("head", None, None))
    out_specs = P(("ctx", "head"), None)
    return jax.shard_map(
        per_device, mesh=mesh, in_specs=in_specs, out_specs=out_specs, check_vma=False
    )
```

```python
import jax
import jax.numpy as jnp
from jax import lax
from jax.experimental import pallas as pl
from jax.experimental.pallas import tpu as pltpu
from jax.sharding import PartitionSpec as P

DC = 512
DR = 64
DV = 128
KBLK = 64
SEL = 8
WIDTH = DC + DR
BAND_TOKENS = 2
BAND = BAND_TOKENS * WIDTH
ROW = BAND + 128
Y, Z, CORES = 8, 8, 2
HEAD_BLOCK = 8
FACTOR = (DV + DR) ** -0.5 * 1.4426950408889634


def attend_kernel(base_ref, selected_ref, q_hbm, k_ref, w_ref, o_ref, keys_ref, q_ref, q_sems):
    heads, tokens, width = q_ref.shape
    bands, per_band, _ = k_ref.shape
    blocks = tokens // KBLK
    half = bands * SEL
    count = BAND_TOKENS * half

    copies = []
    for head in range(heads):
        copy = pltpu.make_async_copy(q_hbm.at[head], q_ref.at[head], q_sems.at[head])
        copy.start()
        copies.append(copy)

    lane = lax.broadcasted_iota(jnp.int32, (1, count), 1)
    slot = lane % SEL
    offset = (lane // SEL) % bands * BAND_TOKENS + lane // half
    biases = []
    for block in range(blocks):
        picked = slice(block * SEL, (block + 1) * SEL)
        for token in range(BAND_TOKENS):
            rows = k_ref[:, picked, token * width : (token + 1) * width]
            keys_ref[block, token * half : (token + 1) * half, :] = rows.reshape(half, width)
        chosen = jnp.full((1, count), -1, jnp.int32)
        for index in range(SEL):
            chosen = jnp.where(slot == index, selected_ref[block, index], chosen)
        place = jnp.where(chosen >= 0, chosen * KBLK + offset, 2**30)
        first = (base_ref[0] + block) * KBLK
        query_place = first + lax.broadcasted_iota(jnp.int32, (KBLK, 1), 0)
        biases.append(jnp.where(place <= query_place, 0.0, -1e30))

    def score(start, block):
        here = slice(block * KBLK, (block + 1) * KBLK)
        queries = q_ref[start : start + HEAD_BLOCK, here, :].reshape(HEAD_BLOCK * KBLK, width)
        return lax.dot_general(
            queries, keys_ref[block], (((1,), (1,)), ((), ())), preferred_element_type=jnp.float32
        )

    def finish(start, block, scores):
        here = slice(block * KBLK, (block + 1) * KBLK)
        scores = scores.reshape(HEAD_BLOCK, KBLK, count) * FACTOR + biases[block][None]
        powered = jnp.exp2(scores - jnp.max(scores, axis=2, keepdims=True))
        total = jnp.sum(powered, axis=2, keepdims=True)
        mixed = lax.dot_general(
            powered.astype(jnp.bfloat16).reshape(HEAD_BLOCK * KBLK, count),
            keys_ref[block][:, :DC],
            (((1,), (0,)), ((), ())),
            preferred_element_type=jnp.float32,
        ).astype(jnp.bfloat16)
        for head in range(HEAD_BLOCK):
            columns = slice((start + head) * DV, (start + head + 1) * DV)
            expanded = jnp.dot(
                mixed[head * KBLK : (head + 1) * KBLK],
                w_ref[start + head],
                preferred_element_type=jnp.float32,
            )
            o_ref[here, columns] = (expanded / total[head]).astype(jnp.bfloat16)

    chunks = [(start, block) for start in range(0, heads, HEAD_BLOCK) for block in range(blocks)]
    waiting = None
    for start, block in chunks:
        if block == 0:
            for copy in copies[start : start + HEAD_BLOCK]:
                copy.wait()
        scores = score(start, block)
        if waiting is not None:
            finish(*waiting)
        waiting = (start, block, scores)
    finish(*waiting)


def attend(base, selected, queries, keys, value_weight):
    heads, tokens, width = queries.shape
    blocks = selected.shape[0]
    vmem = pl.BlockSpec(memory_space=pltpu.VMEM)
    smem = pl.BlockSpec(memory_space=pltpu.SMEM)
    return pl.pallas_call(
        attend_kernel,
        out_shape=jax.ShapeDtypeStruct((tokens, heads * DV), jnp.bfloat16),
        in_specs=[smem, smem, pl.BlockSpec(memory_space=pltpu.HBM), vmem, vmem],
        out_specs=vmem,
        scratch_shapes=[
            pltpu.VMEM((blocks, SEL * KBLK, width), jnp.bfloat16),
            pltpu.VMEM(queries.shape, queries.dtype),
            pltpu.SemaphoreType.DMA((heads,)),
        ],
        compiler_params=pltpu.CompilerParams(vmem_limit_bytes=32 * 2**20),
    )(base, selected, pltpu.with_memory_space_constraint(queries, pltpu.HBM), keys, value_weight)


def spread_kernel(head_ref, selected_ref, latent_ref, out_ref, band_ref, in_sem, out_sem):
    cell, here, row = band_ref.shape
    first = head_ref[0] * (cell * BAND)
    incoming = []
    for place in range(cell):
        columns = pl.ds(pl.multiple_of(first + place * BAND, 128), BAND)
        copy = pltpu.make_async_copy(
            latent_ref.at[:, columns], band_ref.at[place, :, pl.ds(0, BAND)], in_sem.at[place]
        )
        copy.start()
        incoming.append(copy)
    lists = selected_ref[...].astype(jnp.bfloat16)
    for place in range(cell):
        band_ref[place, :, BAND:] = jnp.zeros((here, row - BAND), jnp.bfloat16)
        band_ref[place, :, BAND : BAND + SEL] = lists
    for copy in incoming:
        copy.wait()
    outgoing = []
    for y in range(Y // 2):
        for z in range(Z // 2):
            for dy in range(2):
                half = pl.ds(dy * cell // 2, cell // 2)
                copy = pltpu.make_async_copy(
                    band_ref.at[half], out_ref.at[y, dy, z], out_sem.at[len(outgoing)]
                )
                copy.start()
                outgoing.append(copy)
    for copy in outgoing:
        copy.wait()


def spread_bands(head, selected, latent_cache):
    here = selected.shape[0]
    cell = 4 * CORES
    hbm = pl.BlockSpec(memory_space=pltpu.HBM)
    return pl.pallas_call(
        spread_kernel,
        out_shape=jax.ShapeDtypeStruct((Y // 2, 2, Z // 2, cell // 2, here, ROW), jnp.bfloat16),
        in_specs=[
            pl.BlockSpec(memory_space=pltpu.SMEM),
            pl.BlockSpec(memory_space=pltpu.VMEM),
            hbm,
        ],
        out_specs=hbm,
        scratch_shapes=[
            pltpu.VMEM((cell, here, ROW), jnp.bfloat16),
            pltpu.SemaphoreType.DMA((cell,)),
            pltpu.SemaphoreType.DMA((Y * Z // 2,)),
        ],
    )(head.astype(jnp.int32).reshape(1), selected, latent_cache)


def stage_kernel(raw_hbm, w_hbm, q_hbm, w_ref, raw_ref, q_ref, sems, out_sems):
    heads, tokens, _ = q_ref.shape
    w_copy = pltpu.make_async_copy(w_hbm, w_ref, sems.at[heads])
    w_copy.start()
    copies = []
    for head in range(heads):
        copy = pltpu.make_async_copy(raw_hbm.at[head], raw_ref.at[head], sems.at[head])
        copy.start()
        copies.append(copy)
    same = lax.broadcasted_iota(jnp.int32, (tokens, tokens), 0) == lax.broadcasted_iota(
        jnp.int32, (tokens, tokens), 1
    )
    unit = same.astype(jnp.float32).astype(jnp.bfloat16)
    for head in range(heads):
        copies[head].wait()
        turned = lax.dot_general(
            unit, raw_ref[head], (((1,), (1,)), ((), ())), preferred_element_type=jnp.float32
        )
        q_ref[head] = turned.astype(jnp.bfloat16)
    for head in range(heads):
        copies[head] = pltpu.make_async_copy(q_ref.at[head], q_hbm.at[head], out_sems.at[head])
        copies[head].start()
    for copy in copies:
        copy.wait()
    w_copy.wait()


def stage(queries, value_weight):
    tokens, heads, width = queries.shape
    hbm = pl.BlockSpec(memory_space=pltpu.HBM)
    vmem = pl.BlockSpec(memory_space=pltpu.VMEM)
    raw = queries.transpose(1, 2, 0)
    return pl.pallas_call(
        stage_kernel,
        out_shape=(
            jax.ShapeDtypeStruct((heads, tokens, width), queries.dtype),
            jax.ShapeDtypeStruct(value_weight.shape, value_weight.dtype),
        ),
        in_specs=[hbm, hbm],
        out_specs=(hbm, vmem),
        scratch_shapes=[
            pltpu.VMEM((heads, width, tokens), queries.dtype),
            pltpu.VMEM((heads, tokens, width), queries.dtype),
            pltpu.SemaphoreType.DMA((heads + 1,)),
            pltpu.SemaphoreType.DMA((heads,)),
        ],
        compiler_params=pltpu.CompilerParams(vmem_limit_bytes=16 * 2**20),
        cost_estimate=pl.CostEstimate(flops=10**9, transcendentals=0, bytes_accessed=10 * 2**20),
    )(
        pltpu.with_memory_space_constraint(raw, pltpu.HBM),
        pltpu.with_memory_space_constraint(value_weight, pltpu.HBM),
    )


def fetch_groups(heads):
    groups = []
    for y in range(Y // 2):
        for z in range(Z // 2):
            groups.append([
                (((2 * y + dy) * Z + 2 * z + dz) * CORES + core) * heads + head
                for head in range(heads)
                for dy in range(2)
                for dz in range(2)
                for core in range(CORES)
            ])
    return groups


def per_device(queries, latent_cache, selected, value_weight):
    ctx_size = lax.axis_size("ctx")
    heads = lax.axis_size("head")
    ctx = lax.axis_index("ctx")
    head = lax.axis_index("head")
    here = selected.shape[0]
    cell = 4 * CORES
    bands = heads * cell

    spread = lax.all_to_all(
        spread_bands(head, selected, latent_cache).reshape(ctx_size, here, ROW),
        "ctx",
        split_axis=0,
        concat_axis=0,
        tiled=True,
    )
    table = spread.reshape(ctx_size * here, ROW)

    lists = spread[:, :, BAND : BAND + SEL].reshape(Y // 2, 2, Z // 2, 2, CORES, here, SEL)
    y, z = ctx // (Z * CORES), (ctx // CORES) % Z
    lists = lax.dynamic_slice_in_dim(lists, y // 2, 1, 0)
    lists = lax.dynamic_slice_in_dim(lists, z // 2, 1, 2)
    wanted = lists.astype(jnp.int32).reshape(-1)
    chosen = wanted[:, None] == jnp.arange(ctx_size * here, dtype=jnp.int32)[None, :]
    picked = jnp.dot(
        chosen.astype(jnp.bfloat16), table[:, :BAND], preferred_element_type=jnp.float32
    ).astype(jnp.bfloat16)
    picked = picked.reshape(1, cell, here * SEL, BAND)
    keys = lax.all_to_all(
        jnp.broadcast_to(picked, (heads, cell, here * SEL, BAND)).reshape(bands, here * SEL, BAND),
        ("ctx", "head"),
        split_axis=0,
        concat_axis=0,
        axis_index_groups=fetch_groups(heads),
        tiled=True,
    )

    base = (ctx * here).astype(jnp.int32).reshape(1)
    turned, mapping = stage(queries, value_weight)
    attended = attend(base, selected, turned, keys, mapping)
    return lax.all_to_all(attended, "head", split_axis=0, concat_axis=1, tiled=True)


def solution(mesh):
    in_specs = (P("ctx", "head", None), P("ctx", None), P("ctx", None), P("head", None, None))
    out_specs = P(("ctx", "head"), None)
    return jax.shard_map(
        per_device, mesh=mesh, in_specs=in_specs, out_specs=out_specs, check_vma=False
    )
```

```python
import jax
import jax.numpy as jnp
from jax import lax
from jax.experimental import pallas as pl
from jax.experimental.pallas import tpu as pltpu
from jax.sharding import PartitionSpec as P

DC = 512
DR = 64
DV = 128
KBLK = 64
SEL = 8
WIDTH = DC + DR
BAND_TOKENS = 2
BAND = BAND_TOKENS * WIDTH
ROW = BAND + 128
Y, Z, CORES = 8, 8, 2
FACTOR = (DV + DR) ** -0.5 * 1.4426950408889634


def attend_kernel(low_ref, high_hbm, k_ref, place_ref, w_hbm, o_ref, keys_ref, high_ref, w_ref, sems):
    part, tokens, width = low_ref.shape
    heads = w_ref.shape[0]
    bands, per_band, _ = k_ref.shape
    blocks = tokens // KBLK
    half = bands * SEL
    count = BAND_TOKENS * half

    low, high = pl.ds(0, part), pl.ds(part, part)
    copies = [
        pltpu.make_async_copy(w_hbm.at[low], w_ref.at[low], sems.at[0]),
        pltpu.make_async_copy(high_hbm, high_ref, sems.at[1]),
        pltpu.make_async_copy(w_hbm.at[high], w_ref.at[high], sems.at[2]),
    ]
    for copy in copies:
        copy.start()

    biases = []
    for block in range(blocks):
        picked = slice(block * SEL, (block + 1) * SEL)
        for token in range(BAND_TOKENS):
            rows = k_ref[:, picked, token * width : (token + 1) * width]
            keys_ref[block, token * half : (token + 1) * half, :] = rows.reshape(half, width)
        query_place = lax.broadcasted_iota(jnp.int32, (KBLK, 1), 0)
        biases.append(jnp.where(place_ref[block] <= query_place, 0.0, -1e30))

    def score(group, block):
        here = slice(block * KBLK, (block + 1) * KBLK)
        queries = (high_ref if group else low_ref)[:, here, :].reshape(part * KBLK, width)
        return lax.dot_general(
            queries, keys_ref[block], (((1,), (1,)), ((), ())), preferred_element_type=jnp.float32
        )

    def finish(group, block, scores):
        here = slice(block * KBLK, (block + 1) * KBLK)
        scores = scores.reshape(part, KBLK, count) * FACTOR + biases[block][None]
        powered = jnp.exp2(scores - jnp.max(scores, axis=2, keepdims=True))
        total = jnp.sum(powered, axis=2, keepdims=True)
        mixed = lax.dot_general(
            powered.astype(jnp.bfloat16).reshape(part * KBLK, count),
            keys_ref[block][:, :DC],
            (((1,), (0,)), ((), ())),
            preferred_element_type=jnp.float32,
        ).astype(jnp.bfloat16)
        if block == 0:
            copies[2 if group else 0].wait()
        for index in range(part):
            head = group * part + index
            columns = slice(head * DV, (head + 1) * DV)
            expanded = jnp.dot(
                mixed[index * KBLK : (index + 1) * KBLK],
                w_ref[head],
                preferred_element_type=jnp.float32,
            )
            o_ref[here, columns] = (expanded / total[index]).astype(jnp.bfloat16)

    waiting = None
    for group in range(heads // part):
        for block in range(blocks):
            if group and block == 0:
                copies[1].wait()
            scores = score(group, block)
            if waiting is not None:
                finish(*waiting)
            waiting = (group, block, scores)
    finish(*waiting)


def attend(low, high, keys, place, value_weight):
    part, tokens, width = low.shape
    heads = value_weight.shape[0]
    blocks = tokens // KBLK
    vmem = pl.BlockSpec(memory_space=pltpu.VMEM)
    hbm = pl.BlockSpec(memory_space=pltpu.HBM)
    return pl.pallas_call(
        attend_kernel,
        out_shape=jax.ShapeDtypeStruct((tokens, heads * DV), jnp.bfloat16),
        in_specs=[vmem, hbm, vmem, vmem, hbm],
        out_specs=vmem,
        scratch_shapes=[
            pltpu.VMEM((blocks, SEL * KBLK, width), jnp.bfloat16),
            pltpu.VMEM(high.shape, high.dtype),
            pltpu.VMEM(value_weight.shape, value_weight.dtype),
            pltpu.SemaphoreType.DMA((3,)),
        ],
        compiler_params=pltpu.CompilerParams(vmem_limit_bytes=32 * 2**20),
    )(
        low,
        pltpu.with_memory_space_constraint(high, pltpu.HBM),
        keys,
        place,
        pltpu.with_memory_space_constraint(value_weight, pltpu.HBM),
    )


def spread_kernel(selected_hbm, latent_hbm, out_hbm, band_ref, selected_ref, in_sem, out_sem):
    cell, here, row = band_ref.shape
    first = lax.axis_index("head") * (cell * BAND)
    incoming = [pltpu.make_async_copy(selected_hbm, selected_ref, in_sem.at[cell])]
    for place in range(cell):
        columns = pl.ds(pl.multiple_of(first + place * BAND, 128), BAND)
        incoming.append(
            pltpu.make_async_copy(
                latent_hbm.at[:, columns], band_ref.at[place, :, pl.ds(0, BAND)], in_sem.at[place]
            )
        )
    for copy in incoming:
        copy.start()
    for place in range(cell):
        band_ref[place, :, BAND:] = jnp.zeros((here, row - BAND), jnp.bfloat16)
    incoming[0].wait()
    lists = selected_ref[...].astype(jnp.bfloat16)
    for place in range(cell):
        band_ref[place, :, BAND : BAND + SEL] = lists
    for copy in incoming[1:]:
        copy.wait()
    outgoing = []
    for y in range(Y // 2):
        for z in range(Z // 2):
            for dy in range(2):
                half = pl.ds(dy * cell // 2, cell // 2)
                copy = pltpu.make_async_copy(
                    band_ref.at[half], out_hbm.at[y, dy, z], out_sem.at[len(outgoing)]
                )
                copy.start()
                outgoing.append(copy)
    for copy in outgoing:
        copy.wait()


def spread_bands(selected, latent_cache):
    here = selected.shape[0]
    cell = 4 * CORES
    hbm = pl.BlockSpec(memory_space=pltpu.HBM)
    return pl.pallas_call(
        spread_kernel,
        out_shape=jax.ShapeDtypeStruct((Y // 2, 2, Z // 2, cell // 2, here, ROW), jnp.bfloat16),
        in_specs=[hbm, hbm],
        out_specs=hbm,
        scratch_shapes=[
            pltpu.VMEM((cell, here, ROW), jnp.bfloat16),
            pltpu.VMEM(selected.shape, jnp.int32),
            pltpu.SemaphoreType.DMA((cell + 1,)),
            pltpu.SemaphoreType.DMA((Y * Z // 2,)),
        ],
    )(
        pltpu.with_memory_space_constraint(selected, pltpu.HBM),
        pltpu.with_memory_space_constraint(latent_cache, pltpu.HBM),
    )


def stage_kernel(selected_ref, raw_hbm, low_ref, high_hbm, place_ref, raw_ref, high_ref, sems, out_sem):
    heads, _, tokens = raw_ref.shape
    part = low_ref.shape[0]
    copies = []
    for head in range(heads):
        copy = pltpu.make_async_copy(raw_hbm.at[head], raw_ref.at[head], sems.at[head])
        copy.start()
        copies.append(copy)

    blocks, _, count = place_ref.shape
    lane = lax.broadcasted_iota(jnp.int32, (1, count), 1)
    slot = lane % SEL
    half = count // BAND_TOKENS
    offset = (lane % half) // SEL * BAND_TOKENS + lane // half
    for block in range(blocks):
        chosen = jnp.full((1, count), -1, jnp.int32)
        for index in range(SEL):
            chosen = jnp.where(slot == index, selected_ref[block, index], chosen)
        own = lax.axis_index("ctx") * blocks + block
        place_ref[block] = jnp.where(chosen >= 0, (chosen - own) * KBLK + offset, 2**30)

    same = lax.broadcasted_iota(jnp.int32, (tokens, tokens), 0) == lax.broadcasted_iota(
        jnp.int32, (tokens, tokens), 1
    )
    unit = same.astype(jnp.float32).astype(jnp.bfloat16)
    for head in range(heads):
        copies[head].wait()
        turned = lax.dot_general(
            unit, raw_ref[head], (((1,), (1,)), ((), ())), preferred_element_type=jnp.float32
        ).astype(jnp.bfloat16)
        if head < part:
            low_ref[head] = turned
        else:
            high_ref[head - part] = turned
    copy = pltpu.make_async_copy(high_ref, high_hbm, out_sem)
    copy.start()
    copy.wait()


def stage(selected, queries):
    tokens, heads, width = queries.shape
    blocks = selected.shape[0]
    hbm = pl.BlockSpec(memory_space=pltpu.HBM)
    vmem = pl.BlockSpec(memory_space=pltpu.VMEM)
    group = jax.ShapeDtypeStruct((heads // 2, tokens, width), queries.dtype)
    return pl.pallas_call(
        stage_kernel,
        out_shape=(group, group, jax.ShapeDtypeStruct((blocks, 1, SEL * KBLK), jnp.int32)),
        in_specs=[pl.BlockSpec(memory_space=pltpu.SMEM), hbm],
        out_specs=(vmem, hbm, vmem),
        scratch_shapes=[
            pltpu.VMEM((heads, width, tokens), queries.dtype),
            pltpu.VMEM(group.shape, queries.dtype),
            pltpu.SemaphoreType.DMA((heads,)),
            pltpu.SemaphoreType.DMA,
        ],
        compiler_params=pltpu.CompilerParams(vmem_limit_bytes=16 * 2**20),
        cost_estimate=pl.CostEstimate(flops=10**9, transcendentals=0, bytes_accessed=10 * 2**20),
    )(selected, pltpu.with_memory_space_constraint(queries.transpose(1, 2, 0), pltpu.HBM))


def fetch_groups(heads):
    groups = []
    for y in range(Y // 2):
        for z in range(Z // 2):
            groups.append([
                (((2 * y + dy) * Z + 2 * z + dz) * CORES + core) * heads + head
                for head in range(heads)
                for dy in range(2)
                for dz in range(2)
                for core in range(CORES)
            ])
    return groups


def per_device(queries, latent_cache, selected, value_weight):
    ctx_size = lax.axis_size("ctx")
    heads = lax.axis_size("head")
    ctx = lax.axis_index("ctx")
    here = selected.shape[0]
    cell = 4 * CORES
    bands = heads * cell

    spread = lax.all_to_all(
        spread_bands(selected, latent_cache).reshape(ctx_size, here, ROW),
        "ctx",
        split_axis=0,
        concat_axis=0,
        tiled=True,
    )
    table = spread.reshape(ctx_size * here, ROW)

    lists = spread[:, :, BAND : BAND + SEL].reshape(Y // 2, 2, Z // 2, 2, CORES, here, SEL)
    y, z = ctx // (Z * CORES), (ctx // CORES) % Z
    lists = lax.dynamic_slice_in_dim(lists, y // 2, 1, 0)
    lists = lax.dynamic_slice_in_dim(lists, z // 2, 1, 2)
    wanted = lists.astype(jnp.int32).reshape(-1)
    chosen = wanted[:, None] == jnp.arange(ctx_size * here, dtype=jnp.int32)[None, :]
    picked = jnp.dot(
        chosen.astype(jnp.bfloat16), table[:, :BAND], preferred_element_type=jnp.float32
    ).astype(jnp.bfloat16)
    picked = picked.reshape(1, cell, here * SEL, BAND)
    keys = lax.all_to_all(
        jnp.broadcast_to(picked, (heads, cell, here * SEL, BAND)).reshape(bands, here * SEL, BAND),
        ("ctx", "head"),
        split_axis=0,
        concat_axis=0,
        axis_index_groups=fetch_groups(heads),
        tiled=True,
    )

    low, high, place = stage(selected, queries)
    attended = attend(low, high, keys, place, value_weight)
    return lax.all_to_all(attended, "head", split_axis=0, concat_axis=1, tiled=True)


def solution(mesh):
    in_specs = (P("ctx", "head", None), P("ctx", None), P("ctx", None), P("head", None, None))
    out_specs = P(("ctx", "head"), None)
    return jax.shard_map(
        per_device, mesh=mesh, in_specs=in_specs, out_specs=out_specs, check_vma=False
    )
```

```python
import jax
import jax.numpy as jnp
from jax import lax
from jax.experimental import pallas as pl
from jax.experimental.pallas import tpu as pltpu
from jax.sharding import PartitionSpec as P


DC = 512
DR = 64
DV = 128
KBLK = 64
SEL = 8
WIDTH = DC + DR
BAND_TOKENS = 2
BAND = BAND_TOKENS * WIDTH
ROW = BAND + 128
Y, Z, CORES = 8, 8, 2
FACTOR = (DV + DR) ** -0.5 * 1.4426950408889634


def attend_kernel(q_ref, k_ref, place_ref, w_hbm, o_ref, keys_ref, w_ref, sems):
    heads, tokens, width = q_ref.shape
    part = heads // 2
    bands, _, _ = k_ref.shape
    blocks = tokens // KBLK
    half = bands * SEL
    count = BAND_TOKENS * half

    low, high = pl.ds(0, part), pl.ds(part, part)
    copies = [
        pltpu.make_async_copy(w_hbm.at[low], w_ref.at[low], sems.at[0]),
        pltpu.make_async_copy(w_hbm.at[high], w_ref.at[high], sems.at[1]),
    ]
    for copy in copies:
        copy.start()

    biases = []
    for block in range(blocks):
        picked = slice(block * SEL, (block + 1) * SEL)
        for token in range(BAND_TOKENS):
            rows = k_ref[:, picked, token * width : (token + 1) * width]
            keys_ref[block, token * half : (token + 1) * half, :] = rows.reshape(half, width)
        query_place = lax.broadcasted_iota(jnp.int32, (KBLK, 1), 0)
        biases.append(jnp.where(place_ref[block] <= query_place, 0.0, -1e30))

    def score(group, block):
        here = slice(block * KBLK, (block + 1) * KBLK)
        queries = q_ref[group * part : (group + 1) * part, here, :].reshape(part * KBLK, width)
        return lax.dot_general(
            queries, keys_ref[block], (((1,), (1,)), ((), ())), preferred_element_type=jnp.float32
        )

    def finish(group, block, scores):
        here = slice(block * KBLK, (block + 1) * KBLK)
        scores = scores.reshape(part, KBLK, count) * FACTOR + biases[block][None]
        powered = jnp.exp2(scores - jnp.max(scores, axis=2, keepdims=True))
        total = jnp.sum(powered, axis=2, keepdims=True)
        mixed = lax.dot_general(
            powered.astype(jnp.bfloat16).reshape(part * KBLK, count),
            keys_ref[block][:, :DC],
            (((1,), (0,)), ((), ())),
            preferred_element_type=jnp.float32,
        ).astype(jnp.bfloat16)
        if block == 0:
            copies[group].wait()
        for index in range(part):
            head = group * part + index
            columns = slice(head * DV, (head + 1) * DV)
            expanded = jnp.dot(
                mixed[index * KBLK : (index + 1) * KBLK],
                w_ref[head],
                preferred_element_type=jnp.float32,
            )
            o_ref[here, columns] = (expanded / total[index]).astype(jnp.bfloat16)

    waiting = None
    for group in range(heads // part):
        for block in range(blocks):
            scores = score(group, block)
            if waiting is not None:
                finish(*waiting)
            waiting = (group, block, scores)
    finish(*waiting)


def attend(queries, keys, place, value_weight):
    heads, tokens, width = queries.shape
    blocks = tokens // KBLK
    vmem = pl.BlockSpec(memory_space=pltpu.VMEM)
    return pl.pallas_call(
        attend_kernel,
        out_shape=jax.ShapeDtypeStruct((tokens, heads * DV), jnp.bfloat16),
        in_specs=[vmem, vmem, vmem, pl.BlockSpec(memory_space=pltpu.HBM)],
        out_specs=vmem,
        scratch_shapes=[
            pltpu.VMEM((blocks, SEL * KBLK, width), jnp.bfloat16),
            pltpu.VMEM(value_weight.shape, value_weight.dtype),
            pltpu.SemaphoreType.DMA((2,)),
        ],
        compiler_params=pltpu.CompilerParams(vmem_limit_bytes=32 * 2**20),
    )(queries, keys, place, pltpu.with_memory_space_constraint(value_weight, pltpu.HBM))


def spread_kernel(selected_hbm, latent_hbm, out_hbm, band_ref, selected_ref, in_sem, out_sem):
    cell, here, row = band_ref.shape
    first = lax.axis_index("head") * (cell * BAND)
    incoming = [pltpu.make_async_copy(selected_hbm, selected_ref, in_sem.at[cell])]
    for place in range(cell):
        columns = pl.ds(pl.multiple_of(first + place * BAND, 128), BAND)
        incoming.append(
            pltpu.make_async_copy(
                latent_hbm.at[:, columns], band_ref.at[place, :, pl.ds(0, BAND)], in_sem.at[place]
            )
        )
    for copy in incoming:
        copy.start()
    for place in range(cell):
        band_ref[place, :, BAND:] = jnp.zeros((here, row - BAND), jnp.bfloat16)
    incoming[0].wait()
    lists = selected_ref[...].astype(jnp.bfloat16)
    for place in range(cell):
        band_ref[place, :, BAND : BAND + SEL] = lists
    for copy in incoming[1:]:
        copy.wait()
    outgoing = []
    for y in range(Y // 2):
        for z in range(Z // 2):
            for dy in range(2):
                half = pl.ds(dy * cell // 2, cell // 2)
                copy = pltpu.make_async_copy(
                    band_ref.at[half], out_hbm.at[y, dy, z], out_sem.at[len(outgoing)]
                )
                copy.start()
                outgoing.append(copy)
    for copy in outgoing:
        copy.wait()


def spread_bands(selected, latent_cache):
    here = selected.shape[0]
    cell = 4 * CORES
    hbm = pl.BlockSpec(memory_space=pltpu.HBM)
    return pl.pallas_call(
        spread_kernel,
        out_shape=jax.ShapeDtypeStruct((Y // 2, 2, Z // 2, cell // 2, here, ROW), jnp.bfloat16),
        in_specs=[hbm, hbm],
        out_specs=hbm,
        scratch_shapes=[
            pltpu.VMEM((cell, here, ROW), jnp.bfloat16),
            pltpu.VMEM(selected.shape, jnp.int32),
            pltpu.SemaphoreType.DMA((cell + 1,)),
            pltpu.SemaphoreType.DMA((Y * Z // 2,)),
        ],
    )(
        pltpu.with_memory_space_constraint(selected, pltpu.HBM),
        pltpu.with_memory_space_constraint(latent_cache, pltpu.HBM),
    )


def stage_kernel(selected_ref, raw_hbm, q_ref, place_ref, raw_ref, sems):
    heads, _, tokens = raw_ref.shape
    copies = []
    for head in range(heads):
        copy = pltpu.make_async_copy(raw_hbm.at[head], raw_ref.at[head], sems.at[head])
        copy.start()
        copies.append(copy)

    blocks, _, count = place_ref.shape
    lane = lax.broadcasted_iota(jnp.int32, (1, count), 1)
    slot = lane % SEL
    half = count // BAND_TOKENS
    offset = (lane % half) // SEL * BAND_TOKENS + lane // half
    for block in range(blocks):
        chosen = jnp.full((1, count), -1, jnp.int32)
        for index in range(SEL):
            chosen = jnp.where(slot == index, selected_ref[block, index], chosen)
        own = lax.axis_index("ctx") * blocks + block
        place_ref[block] = jnp.where(chosen >= 0, (chosen - own) * KBLK + offset, 2**30)

    same = lax.broadcasted_iota(jnp.int32, (tokens, tokens), 0) == lax.broadcasted_iota(
        jnp.int32, (tokens, tokens), 1
    )
    unit = same.astype(jnp.float32).astype(jnp.bfloat16)
    for head in range(heads):
        copies[head].wait()
        turned = lax.dot_general(
            unit, raw_ref[head], (((1,), (1,)), ((), ())), preferred_element_type=jnp.float32
        )
        q_ref[head] = turned.astype(jnp.bfloat16)


def stage(selected, queries):
    tokens, heads, width = queries.shape
    blocks = selected.shape[0]
    hbm = pl.BlockSpec(memory_space=pltpu.HBM)
    vmem = pl.BlockSpec(memory_space=pltpu.VMEM)
    return pl.pallas_call(
        stage_kernel,
        out_shape=(
            jax.ShapeDtypeStruct((heads, tokens, width), queries.dtype),
            jax.ShapeDtypeStruct((blocks, 1, SEL * KBLK), jnp.int32),
        ),
        in_specs=[pl.BlockSpec(memory_space=pltpu.SMEM), hbm],
        out_specs=(vmem, vmem),
        scratch_shapes=[
            pltpu.VMEM((heads, width, tokens), queries.dtype),
            pltpu.SemaphoreType.DMA((heads,)),
        ],
        compiler_params=pltpu.CompilerParams(vmem_limit_bytes=16 * 2**20),
        cost_estimate=pl.CostEstimate(flops=10**9, transcendentals=0, bytes_accessed=10 * 2**20),
    )(selected, pltpu.with_memory_space_constraint(queries.transpose(1, 2, 0), pltpu.HBM))


def pick_kernel(wanted_ref, table_ref, out_ref):
    blocks = table_ref.shape[0] * table_ref.shape[1]
    table = table_ref[:, :, :BAND].reshape(blocks, BAND)
    chosen = wanted_ref[...] == lax.broadcasted_iota(jnp.int32, (blocks, 1), 0)
    picked = lax.dot_general(
        chosen.astype(jnp.float32).astype(jnp.bfloat16),
        table,
        (((0,), (0,)), ((), ())),
        preferred_element_type=jnp.float32,
    ).astype(jnp.bfloat16)
    for head in range(out_ref.shape[0]):
        out_ref[head] = picked


def pick(wanted, table, heads):
    vmem = pl.BlockSpec(memory_space=pltpu.VMEM)
    return pl.pallas_call(
        pick_kernel,
        out_shape=jax.ShapeDtypeStruct((heads, wanted.shape[1], BAND), table.dtype),
        in_specs=[vmem, vmem],
        out_specs=vmem,
        compiler_params=pltpu.CompilerParams(vmem_limit_bytes=16 * 2**20),
    )(wanted, table)


def fetch_groups(heads):
    groups = []
    for y in range(Y // 2):
        for z in range(Z // 2):
            groups.append([
                (((2 * y + dy) * Z + 2 * z + dz) * CORES + core) * heads + head
                for head in range(heads)
                for dy in range(2)
                for dz in range(2)
                for core in range(CORES)
            ])
    return groups


def per_device(queries, latent_cache, selected, value_weight):
    ctx_size = lax.axis_size("ctx")
    heads = lax.axis_size("head")
    ctx = lax.axis_index("ctx")
    here = selected.shape[0]
    cell = 4 * CORES
    bands = heads * cell

    spread = lax.all_to_all(
        spread_bands(selected, latent_cache).reshape(ctx_size, here, ROW),
        "ctx",
        split_axis=0,
        concat_axis=0,
        tiled=True,
    )
    turned, place = stage(selected, queries)
    lists = spread[:, :, BAND : BAND + SEL].reshape(Y // 2, 2, Z // 2, 2, CORES, here, SEL)
    y, z = ctx // (Z * CORES), (ctx // CORES) % Z
    lists = lax.dynamic_slice_in_dim(lists, y // 2, 1, 0)
    lists = lax.dynamic_slice_in_dim(lists, z // 2, 1, 2)
    wanted = lists.astype(jnp.int32).reshape(-1)
    keys = lax.all_to_all(
        pick(wanted.reshape(1, -1), spread, heads).reshape(bands, here * SEL, BAND),
        ("ctx", "head"),
        split_axis=0,
        concat_axis=0,
        axis_index_groups=fetch_groups(heads),
        tiled=True,
    )
    attended = attend(turned, keys, place, value_weight)
    return lax.all_to_all(attended, "head", split_axis=0, concat_axis=1, tiled=True)


def solution(mesh):
    in_specs = (P("ctx", "head", None), P("ctx", None), P("ctx", None), P("head", None, None))
    out_specs = P(("ctx", "head"), None)
    return jax.shard_map(
        per_device, mesh=mesh, in_specs=in_specs, out_specs=out_specs, check_vma=False
    )
```

```python
import jax
import jax.numpy as jnp
from jax import lax
from jax.experimental import pallas as pl
from jax.experimental.pallas import tpu as pltpu
from jax.sharding import PartitionSpec as P


DC = 512
DR = 64
DV = 128
KBLK = 64
SEL = 8
WIDTH = DC + DR
BAND_TOKENS = 2
BAND = BAND_TOKENS * WIDTH
LANES = 128
ROW = BAND + LANES
Y, Z, CORES = 8, 8, 2
FACTOR = (DV + DR) ** -0.5 * 1.4426950408889634


def attend_kernel(
    q_ref, k_ref, own_ref, place_ref, w_hbm, o_ref, keys_ref, w_ref, plain_ref, wide_ref, sems
):
    heads, tokens, width = q_ref.shape
    part = heads // 2
    bands = k_ref.shape[0]
    blocks = tokens // KBLK
    half = bands * SEL
    count = BAND_TOKENS * half
    others = SEL - 1

    low, high = pl.ds(0, part), pl.ds(part, part)
    copies = [
        pltpu.make_async_copy(w_hbm.at[low], w_ref.at[low], sems.at[0]),
        pltpu.make_async_copy(w_hbm.at[high], w_ref.at[high], sems.at[1]),
    ]
    for copy in copies:
        copy.start()

    plain_ref[...] = k_ref[...].astype(jnp.float32)
    biases = []
    for block in range(blocks):
        for tile in range(BAND // LANES):
            first = (tile * blocks + block) * others
            rows = plain_ref[:, first : first + SEL, :].reshape(half, LANES)
            wide_ref[tile * half : (tile + 1) * half, :] = rows
            wide_ref[pl.ds(tile * half + others, bands, stride=SEL), :] = own_ref[
                block, :, tile * LANES : (tile + 1) * LANES
            ]
        whole = jnp.concatenate(
            [wide_ref[tile * half : (tile + 1) * half, :] for tile in range(BAND // LANES)], axis=1
        ).astype(jnp.bfloat16)
        for token in range(BAND_TOKENS):
            keys_ref[block, token * half : (token + 1) * half, :] = whole[
                :, token * width : (token + 1) * width
            ]
        query_place = lax.broadcasted_iota(jnp.int32, (KBLK, 1), 0)
        biases.append(jnp.where(place_ref[block] <= query_place, 0.0, -1e30))

    def score(group, block):
        here = slice(block * KBLK, (block + 1) * KBLK)
        queries = q_ref[group * part : (group + 1) * part, here, :].reshape(part * KBLK, width)
        return lax.dot_general(
            queries, keys_ref[block], (((1,), (1,)), ((), ())), preferred_element_type=jnp.float32
        )

    def finish(group, block, scores):
        here = slice(block * KBLK, (block + 1) * KBLK)
        scores = scores.reshape(part, KBLK, count) * FACTOR + biases[block][None]
        powered = jnp.exp2(scores - jnp.max(scores, axis=2, keepdims=True))
        total = jnp.sum(powered, axis=2, keepdims=True)
        mixed = lax.dot_general(
            powered.astype(jnp.bfloat16).reshape(part * KBLK, count),
            keys_ref[block][:, :DC],
            (((1,), (0,)), ((), ())),
            preferred_element_type=jnp.float32,
        ).astype(jnp.bfloat16)
        if block == 0:
            copies[group].wait()
        for index in range(part):
            head = group * part + index
            columns = slice(head * DV, (head + 1) * DV)
            expanded = jnp.dot(
                mixed[index * KBLK : (index + 1) * KBLK],
                w_ref[head],
                preferred_element_type=jnp.float32,
            )
            o_ref[here, columns] = (expanded / total[index]).astype(jnp.bfloat16)

    waiting = None
    for group in range(heads // part):
        for block in range(blocks):
            scores = score(group, block)
            if waiting is not None:
                finish(*waiting)
            waiting = (group, block, scores)
    finish(*waiting)


def attend(queries, keys, own, place, value_weight):
    heads, tokens, width = queries.shape
    blocks = tokens // KBLK
    vmem = pl.BlockSpec(memory_space=pltpu.VMEM)
    return pl.pallas_call(
        attend_kernel,
        out_shape=jax.ShapeDtypeStruct((tokens, heads * DV), jnp.bfloat16),
        in_specs=[vmem, vmem, vmem, vmem, pl.BlockSpec(memory_space=pltpu.HBM)],
        out_specs=vmem,
        scratch_shapes=[
            pltpu.VMEM((blocks, SEL * KBLK, width), jnp.bfloat16),
            pltpu.VMEM(value_weight.shape, value_weight.dtype),
            pltpu.VMEM(keys.shape, jnp.float32),
            pltpu.VMEM((BAND // LANES * keys.shape[0] * SEL, LANES), jnp.float32),
            pltpu.SemaphoreType.DMA((2,)),
        ],
        compiler_params=pltpu.CompilerParams(vmem_limit_bytes=32 * 2**20),
    )(queries, keys, own, place, pltpu.with_memory_space_constraint(value_weight, pltpu.HBM))


def spread_kernel(selected_hbm, latent_hbm, out_hbm, band_ref, selected_ref, in_sem, out_sem):
    cell, here, row = band_ref.shape
    first = lax.axis_index("head") * (cell * BAND)
    incoming = [pltpu.make_async_copy(selected_hbm, selected_ref, in_sem.at[cell])]
    for place in range(cell):
        columns = pl.ds(pl.multiple_of(first + place * BAND, 128), BAND)
        incoming.append(
            pltpu.make_async_copy(
                latent_hbm.at[:, columns], band_ref.at[place, :, pl.ds(0, BAND)], in_sem.at[place]
            )
        )
    for copy in incoming:
        copy.start()
    for place in range(cell):
        band_ref[place, :, BAND:] = jnp.zeros((here, row - BAND), jnp.bfloat16)
    incoming[0].wait()
    lists = selected_ref[...].astype(jnp.bfloat16)
    for place in range(cell):
        band_ref[place, :, BAND : BAND + SEL] = lists
    for copy in incoming[1:]:
        copy.wait()
    outgoing = []
    for y in range(Y // 2):
        for z in range(Z // 2):
            for dy in range(2):
                half = pl.ds(dy * cell // 2, cell // 2)
                copy = pltpu.make_async_copy(
                    band_ref.at[half], out_hbm.at[y, dy, z], out_sem.at[len(outgoing)]
                )
                copy.start()
                outgoing.append(copy)
    for copy in outgoing:
        copy.wait()


def spread_bands(selected, latent_cache):
    here = selected.shape[0]
    cell = 4 * CORES
    hbm = pl.BlockSpec(memory_space=pltpu.HBM)
    return pl.pallas_call(
        spread_kernel,
        out_shape=jax.ShapeDtypeStruct((Y // 2, 2, Z // 2, cell // 2, here, ROW), jnp.bfloat16),
        in_specs=[hbm, hbm],
        out_specs=hbm,
        scratch_shapes=[
            pltpu.VMEM((cell, here, ROW), jnp.bfloat16),
            pltpu.VMEM(selected.shape, jnp.int32),
            pltpu.SemaphoreType.DMA((cell + 1,)),
            pltpu.SemaphoreType.DMA((Y * Z // 2,)),
        ],
    )(
        pltpu.with_memory_space_constraint(selected, pltpu.HBM),
        pltpu.with_memory_space_constraint(latent_cache, pltpu.HBM),
    )


def stage_kernel(
    selected_ref, raw_hbm, latent_hbm, q_ref, place_ref, own_ref, raw_ref, latent_ref, sems, own_sem
):
    heads, _, tokens = raw_ref.shape
    own_copy = pltpu.make_async_copy(latent_hbm, latent_ref, own_sem)
    own_copy.start()
    copies = []
    for head in range(heads):
        copy = pltpu.make_async_copy(raw_hbm.at[head], raw_ref.at[head], sems.at[head])
        copy.start()
        copies.append(copy)

    blocks, _, count = place_ref.shape
    lane = lax.broadcasted_iota(jnp.int32, (1, count), 1)
    slot = lane % SEL
    half = count // BAND_TOKENS
    offset = (lane % half) // SEL * BAND_TOKENS + lane // half
    for block in range(blocks):
        chosen = jnp.full((1, count), -1, jnp.int32)
        for index in range(SEL):
            position = (index + SEL - 1) % SEL
            chosen = jnp.where(slot == position, selected_ref[block, index], chosen)
        own = lax.axis_index("ctx") * blocks + block
        place_ref[block] = jnp.where(chosen >= 0, (chosen - own) * KBLK + offset, 2**30)

    same = lax.broadcasted_iota(jnp.int32, (tokens, tokens), 0) == lax.broadcasted_iota(
        jnp.int32, (tokens, tokens), 1
    )
    unit = same.astype(jnp.float32).astype(jnp.bfloat16)
    for head in range(heads):
        copies[head].wait()
        turned = lax.dot_general(
            unit, raw_ref[head], (((1,), (1,)), ((), ())), preferred_element_type=jnp.float32
        )
        q_ref[head] = turned.astype(jnp.bfloat16)
    own_copy.wait()
    for band in range(own_ref.shape[1]):
        rows = latent_ref[:, band * BAND : (band + 1) * BAND].astype(jnp.float32)
        for block in range(blocks):
            own_ref[block, band : band + 1, :] = rows[block : block + 1]


def stage(selected, queries, latent_cache):
    tokens, heads, width = queries.shape
    blocks = selected.shape[0]
    hbm = pl.BlockSpec(memory_space=pltpu.HBM)
    vmem = pl.BlockSpec(memory_space=pltpu.VMEM)
    return pl.pallas_call(
        stage_kernel,
        out_shape=(
            jax.ShapeDtypeStruct((heads, tokens, width), queries.dtype),
            jax.ShapeDtypeStruct((blocks, 1, SEL * KBLK), jnp.int32),
            jax.ShapeDtypeStruct((blocks, KBLK // BAND_TOKENS, BAND), jnp.float32),
        ),
        in_specs=[pl.BlockSpec(memory_space=pltpu.SMEM), hbm, hbm],
        out_specs=(vmem, vmem, vmem),
        scratch_shapes=[
            pltpu.VMEM((heads, width, tokens), queries.dtype),
            pltpu.VMEM(latent_cache.shape, latent_cache.dtype),
            pltpu.SemaphoreType.DMA((heads,)),
            pltpu.SemaphoreType.DMA,
        ],
        compiler_params=pltpu.CompilerParams(vmem_limit_bytes=16 * 2**20),
        cost_estimate=pl.CostEstimate(flops=10**9, transcendentals=0, bytes_accessed=10 * 2**20),
    )(
        selected,
        pltpu.with_memory_space_constraint(queries.transpose(1, 2, 0), pltpu.HBM),
        pltpu.with_memory_space_constraint(latent_cache, pltpu.HBM),
    )


def pick_kernel(wanted_ref, table_ref, out_ref, packed_ref):
    blocks = table_ref.shape[0] * table_ref.shape[1]
    heads, cell, rows, _ = out_ref.shape
    table = table_ref[:, :, :BAND].reshape(blocks, BAND)
    chosen = wanted_ref[...] == lax.broadcasted_iota(jnp.int32, (blocks, 1), 0)
    picked = lax.dot_general(
        chosen.astype(jnp.float32).astype(jnp.bfloat16),
        table,
        (((0,), (0,)), ((), ())),
        preferred_element_type=jnp.float32,
    )
    tiles = BAND // LANES
    count = rows // tiles
    step = picked.shape[0] // cell
    packed_ref[:, tiles * count :, :] = jnp.zeros((cell, rows - tiles * count, LANES), jnp.float32)
    for place in range(cell):
        for tile in range(tiles):
            packed_ref[place, tile * count : (tile + 1) * count, :] = picked[
                place * step : place * step + count, tile * LANES : (tile + 1) * LANES
            ]
    packed = packed_ref[...].astype(out_ref.dtype)
    for head in range(heads):
        out_ref[head] = packed


def pick(wanted, table, heads):
    cell, count = wanted.shape
    step = -(-count // 8) * 8
    rows = -(-count * (BAND // LANES) // 8) * 8
    wanted = jnp.pad(wanted, ((0, 0), (0, step - count)), constant_values=-1).reshape(1, -1)
    vmem = pl.BlockSpec(memory_space=pltpu.VMEM)
    return pl.pallas_call(
        pick_kernel,
        out_shape=jax.ShapeDtypeStruct((heads, cell, rows, LANES), table.dtype),
        in_specs=[vmem, vmem],
        out_specs=vmem,
        scratch_shapes=[pltpu.VMEM((cell, rows, LANES), jnp.float32)],
        compiler_params=pltpu.CompilerParams(vmem_limit_bytes=16 * 2**20),
    )(wanted, table)


def fetch_groups(heads):
    groups = []
    for y in range(Y // 2):
        for z in range(Z // 2):
            groups.append([
                (((2 * y + dy) * Z + 2 * z + dz) * CORES + core) * heads + head
                for head in range(heads)
                for dy in range(2)
                for dz in range(2)
                for core in range(CORES)
            ])
    return groups


def per_device(queries, latent_cache, selected, value_weight):
    ctx_size = lax.axis_size("ctx")
    heads = lax.axis_size("head")
    ctx = lax.axis_index("ctx")
    here = selected.shape[0]
    cell = 4 * CORES
    bands = heads * cell

    spread = lax.all_to_all(
        spread_bands(selected, latent_cache).reshape(ctx_size, here, ROW),
        "ctx",
        split_axis=0,
        concat_axis=0,
        tiled=True,
    )
    turned, place, own = stage(selected, queries, latent_cache)
    lists = spread[:, :, BAND : BAND + SEL].reshape(Y // 2, 2, Z // 2, 2, CORES, here, SEL)
    y, z = ctx // (Z * CORES), (ctx // CORES) % Z
    lists = lax.dynamic_slice_in_dim(lists, y // 2, 1, 0)
    lists = lax.dynamic_slice_in_dim(lists, z // 2, 1, 2)
    wanted = lists.astype(jnp.int32)[..., 1:].reshape(cell, -1)
    rows = pick(wanted, spread, heads)
    keys = lax.all_to_all(
        rows.reshape(bands, rows.shape[2], LANES),
        ("ctx", "head"),
        split_axis=0,
        concat_axis=0,
        axis_index_groups=fetch_groups(heads),
        tiled=True,
    )
    attended = attend(turned, keys, own, place, value_weight)
    return lax.all_to_all(attended, "head", split_axis=0, concat_axis=1, tiled=True)


def solution(mesh):
    in_specs = (P("ctx", "head", None), P("ctx", None), P("ctx", None), P("head", None, None))
    out_specs = P(("ctx", "head"), None)
    return jax.shard_map(
        per_device, mesh=mesh, in_specs=in_specs, out_specs=out_specs, check_vma=False
    )
```

```python
import jax
import jax.numpy as jnp
from jax import lax
from jax.experimental import pallas as pl
from jax.experimental.pallas import tpu as pltpu
from jax.sharding import PartitionSpec as P


DC = 512
DR = 64
DV = 128
KBLK = 64
SEL = 8
WIDTH = DC + DR
BAND_TOKENS = 2
BAND = BAND_TOKENS * WIDTH
LANES = 128
Y, Z, CORES = 8, 8, 2
FACTOR = (DV + DR) ** -0.5 * 1.4426950408889634


def attend_kernel(
    q_ref, k_ref, own_ref, place_ref, w_hbm, o_ref, keys_ref, w_ref, plain_ref, wide_ref, sems
):
    heads, tokens, width = q_ref.shape
    part = heads // 2
    bands = k_ref.shape[0]
    blocks = tokens // KBLK
    half = bands * SEL
    count = BAND_TOKENS * half
    others = SEL - 1

    low, high = pl.ds(0, part), pl.ds(part, part)
    copies = [
        pltpu.make_async_copy(w_hbm.at[low], w_ref.at[low], sems.at[0]),
        pltpu.make_async_copy(w_hbm.at[high], w_ref.at[high], sems.at[1]),
    ]
    for copy in copies:
        copy.start()

    plain_ref[...] = k_ref[...].astype(jnp.float32)
    biases = []
    for block in range(blocks):
        for tile in range(BAND // LANES):
            first = (tile * blocks + block) * others
            rows = plain_ref[:, first : first + SEL, :].reshape(half, LANES)
            wide_ref[tile * half : (tile + 1) * half, :] = rows
            wide_ref[pl.ds(tile * half + others, bands, stride=SEL), :] = own_ref[
                block, :, tile * LANES : (tile + 1) * LANES
            ]
        whole = jnp.concatenate(
            [wide_ref[tile * half : (tile + 1) * half, :] for tile in range(BAND // LANES)], axis=1
        ).astype(jnp.bfloat16)
        for token in range(BAND_TOKENS):
            keys_ref[block, token * half : (token + 1) * half, :] = whole[
                :, token * width : (token + 1) * width
            ]
        query_place = lax.broadcasted_iota(jnp.int32, (KBLK, 1), 0)
        biases.append(jnp.where(place_ref[block] <= query_place, 0.0, -1e30))

    def score(group, block):
        here = slice(block * KBLK, (block + 1) * KBLK)
        queries = q_ref[group * part : (group + 1) * part, here, :].reshape(part * KBLK, width)
        return lax.dot_general(
            queries, keys_ref[block], (((1,), (1,)), ((), ())), preferred_element_type=jnp.float32
        )

    def finish(group, block, scores):
        here = slice(block * KBLK, (block + 1) * KBLK)
        scores = scores.reshape(part, KBLK, count) * FACTOR + biases[block][None]
        powered = jnp.exp2(scores - jnp.max(scores, axis=2, keepdims=True))
        total = jnp.sum(powered, axis=2, keepdims=True)
        mixed = lax.dot_general(
            powered.astype(jnp.bfloat16).reshape(part * KBLK, count),
            keys_ref[block][:, :DC],
            (((1,), (0,)), ((), ())),
            preferred_element_type=jnp.float32,
        ).astype(jnp.bfloat16)
        if block == 0:
            copies[group].wait()
        for index in range(part):
            head = group * part + index
            columns = slice(head * DV, (head + 1) * DV)
            expanded = jnp.dot(
                mixed[index * KBLK : (index + 1) * KBLK],
                w_ref[head],
                preferred_element_type=jnp.float32,
            )
            o_ref[here, columns] = (expanded / total[index]).astype(jnp.bfloat16)

    waiting = None
    for group in range(heads // part):
        for block in range(blocks):
            scores = score(group, block)
            if waiting is not None:
                finish(*waiting)
            waiting = (group, block, scores)
    finish(*waiting)


def attend(queries, keys, own, place, value_weight):
    heads, tokens, width = queries.shape
    blocks = tokens // KBLK
    vmem = pl.BlockSpec(memory_space=pltpu.VMEM)
    return pl.pallas_call(
        attend_kernel,
        out_shape=jax.ShapeDtypeStruct((tokens, heads * DV), jnp.bfloat16),
        in_specs=[vmem, vmem, vmem, vmem, pl.BlockSpec(memory_space=pltpu.HBM)],
        out_specs=vmem,
        scratch_shapes=[
            pltpu.VMEM((blocks, SEL * KBLK, width), jnp.bfloat16),
            pltpu.VMEM(value_weight.shape, value_weight.dtype),
            pltpu.VMEM(keys.shape, jnp.float32),
            pltpu.VMEM((BAND // LANES * keys.shape[0] * SEL, LANES), jnp.float32),
            pltpu.SemaphoreType.DMA((2,)),
        ],
        compiler_params=pltpu.CompilerParams(vmem_limit_bytes=32 * 2**20),
    )(queries, keys, own, place, pltpu.with_memory_space_constraint(value_weight, pltpu.HBM))


def spread_kernel(latent_hbm, out_hbm, band_ref, in_sem, out_sem):
    cell = band_ref.shape[0]
    first = lax.axis_index("head") * (cell * BAND)
    incoming = []
    for place in range(cell):
        columns = pl.ds(pl.multiple_of(first + place * BAND, 128), BAND)
        incoming.append(
            pltpu.make_async_copy(
                latent_hbm.at[:, columns], band_ref.at[place], in_sem.at[place]
            )
        )
    for copy in incoming:
        copy.start()
    for copy in incoming:
        copy.wait()
    outgoing = []
    for y in range(Y // 2):
        for z in range(Z // 2):
            for dy in range(2):
                half = pl.ds(dy * cell // 2, cell // 2)
                copy = pltpu.make_async_copy(
                    band_ref.at[half], out_hbm.at[y, dy, z], out_sem.at[len(outgoing)]
                )
                copy.start()
                outgoing.append(copy)
    for copy in outgoing:
        copy.wait()


def spread_bands(latent_cache):
    here = latent_cache.shape[0]
    cell = 4 * CORES
    hbm = pl.BlockSpec(memory_space=pltpu.HBM)
    return pl.pallas_call(
        spread_kernel,
        out_shape=jax.ShapeDtypeStruct((Y // 2, 2, Z // 2, cell // 2, here, BAND), jnp.bfloat16),
        in_specs=[hbm],
        out_specs=hbm,
        scratch_shapes=[
            pltpu.VMEM((cell, here, BAND), jnp.bfloat16),
            pltpu.SemaphoreType.DMA((cell,)),
            pltpu.SemaphoreType.DMA((Y * Z // 2,)),
        ],
    )(pltpu.with_memory_space_constraint(latent_cache, pltpu.HBM))


def stage_kernel(
    selected_ref, raw_hbm, latent_hbm, q_ref, place_ref, own_ref, raw_ref, latent_ref, sems, own_sem
):
    heads, _, tokens = raw_ref.shape
    own_copy = pltpu.make_async_copy(latent_hbm, latent_ref, own_sem)
    own_copy.start()
    copies = []
    for head in range(heads):
        copy = pltpu.make_async_copy(raw_hbm.at[head], raw_ref.at[head], sems.at[head])
        copy.start()
        copies.append(copy)

    blocks, _, count = place_ref.shape
    lane = lax.broadcasted_iota(jnp.int32, (1, count), 1)
    slot = lane % SEL
    half = count // BAND_TOKENS
    offset = (lane % half) // SEL * BAND_TOKENS + lane // half
    for block in range(blocks):
        chosen = jnp.full((1, count), -1, jnp.int32)
        for index in range(SEL):
            position = (index + SEL - 1) % SEL
            chosen = jnp.where(slot == position, selected_ref[block, index], chosen)
        own = lax.axis_index("ctx") * blocks + block
        place_ref[block] = jnp.where(chosen >= 0, (chosen - own) * KBLK + offset, 2**30)

    same = lax.broadcasted_iota(jnp.int32, (tokens, tokens), 0) == lax.broadcasted_iota(
        jnp.int32, (tokens, tokens), 1
    )
    unit = same.astype(jnp.float32).astype(jnp.bfloat16)
    for head in range(heads):
        copies[head].wait()
        turned = lax.dot_general(
            unit, raw_ref[head], (((1,), (1,)), ((), ())), preferred_element_type=jnp.float32
        )
        q_ref[head] = turned.astype(jnp.bfloat16)
    own_copy.wait()
    for band in range(own_ref.shape[1]):
        rows = latent_ref[:, band * BAND : (band + 1) * BAND].astype(jnp.float32)
        for block in range(blocks):
            own_ref[block, band : band + 1, :] = rows[block : block + 1]


def stage(selected, queries, latent_cache):
    tokens, heads, width = queries.shape
    blocks = selected.shape[0]
    hbm = pl.BlockSpec(memory_space=pltpu.HBM)
    vmem = pl.BlockSpec(memory_space=pltpu.VMEM)
    return pl.pallas_call(
        stage_kernel,
        out_shape=(
            jax.ShapeDtypeStruct((heads, tokens, width), queries.dtype),
            jax.ShapeDtypeStruct((blocks, 1, SEL * KBLK), jnp.int32),
            jax.ShapeDtypeStruct((blocks, KBLK // BAND_TOKENS, BAND), jnp.float32),
        ),
        in_specs=[pl.BlockSpec(memory_space=pltpu.SMEM), hbm, hbm],
        out_specs=(vmem, vmem, vmem),
        scratch_shapes=[
            pltpu.VMEM((heads, width, tokens), queries.dtype),
            pltpu.VMEM(latent_cache.shape, latent_cache.dtype),
            pltpu.SemaphoreType.DMA((heads,)),
            pltpu.SemaphoreType.DMA,
        ],
        compiler_params=pltpu.CompilerParams(vmem_limit_bytes=16 * 2**20),
        cost_estimate=pl.CostEstimate(flops=10**9, transcendentals=0, bytes_accessed=10 * 2**20),
    )(
        pltpu.with_memory_space_constraint(selected, pltpu.HBM),
        pltpu.with_memory_space_constraint(queries.transpose(1, 2, 0), pltpu.HBM),
        pltpu.with_memory_space_constraint(latent_cache, pltpu.HBM),
    )


def pick_kernel(wanted_ref, table_ref, out_ref, packed_ref):
    blocks = table_ref.shape[0] * table_ref.shape[1]
    heads, cell, rows, _ = out_ref.shape
    table = table_ref[...].reshape(blocks, BAND)
    chosen = wanted_ref[...] == lax.broadcasted_iota(jnp.int32, (blocks, 1), 0)
    picked = lax.dot_general(
        chosen.astype(jnp.float32).astype(jnp.bfloat16),
        table,
        (((0,), (0,)), ((), ())),
        preferred_element_type=jnp.float32,
    )
    tiles = BAND // LANES
    count = rows // tiles
    step = picked.shape[0] // cell
    packed_ref[:, tiles * count :, :] = jnp.zeros((cell, rows - tiles * count, LANES), jnp.float32)
    for place in range(cell):
        for tile in range(tiles):
            packed_ref[place, tile * count : (tile + 1) * count, :] = picked[
                place * step : place * step + count, tile * LANES : (tile + 1) * LANES
            ]
    packed = packed_ref[...].astype(out_ref.dtype)
    for head in range(heads):
        out_ref[head] = packed


def pick(wanted, table, heads):
    cell, count = wanted.shape
    step = -(-count // 8) * 8
    rows = -(-count * (BAND // LANES) // 8) * 8
    wanted = jnp.pad(wanted, ((0, 0), (0, step - count)), constant_values=-1).reshape(1, -1)
    vmem = pl.BlockSpec(memory_space=pltpu.VMEM)
    return pl.pallas_call(
        pick_kernel,
        out_shape=jax.ShapeDtypeStruct((heads, cell, rows, LANES), table.dtype),
        in_specs=[vmem, vmem],
        out_specs=vmem,
        scratch_shapes=[pltpu.VMEM((cell, rows, LANES), jnp.float32)],
        compiler_params=pltpu.CompilerParams(vmem_limit_bytes=16 * 2**20),
    )(wanted, table)


def fetch_groups(heads):
    groups = []
    for y in range(Y // 2):
        for z in range(Z // 2):
            groups.append([
                (((2 * y + dy) * Z + 2 * z + dz) * CORES + core) * heads + head
                for head in range(heads)
                for dy in range(2)
                for dz in range(2)
                for core in range(CORES)
            ])
    return groups


def per_device(queries, latent_cache, selected, value_weight):
    ctx_size = lax.axis_size("ctx")
    heads = lax.axis_size("head")
    ctx = lax.axis_index("ctx")
    here = selected.shape[0]
    cell = 4 * CORES
    bands = heads * cell

    spread = lax.all_to_all(
        spread_bands(latent_cache).reshape(ctx_size, here, BAND),
        "ctx",
        split_axis=0,
        concat_axis=0,
        tiled=True,
    )
    turned, place, own = stage(selected, queries, latent_cache)

    lists = selected[None]
    for stride in (1, CORES, Z * CORES):
        other = lax.ppermute(lists, "ctx", [(i, i ^ stride) for i in range(ctx_size)])
        first = (ctx // stride) % 2 == 0
        low, high = jnp.where(first, lists, other), jnp.where(first, other, lists)
        lists = jnp.concatenate([low, high], axis=0)
    wanted = lists[:, :, 1:].reshape(cell, -1)
    rows = pick(wanted, spread, heads)
    keys = lax.all_to_all(
        rows.reshape(bands, rows.shape[2], LANES),
        ("ctx", "head"),
        split_axis=0,
        concat_axis=0,
        axis_index_groups=fetch_groups(heads),
        tiled=True,
    )
    attended = attend(turned, keys, own, place, value_weight)
    return lax.all_to_all(attended, "head", split_axis=0, concat_axis=1, tiled=True)


def solution(mesh):
    in_specs = (P("ctx", "head", None), P("ctx", None), P("ctx", None), P("head", None, None))
    out_specs = P(("ctx", "head"), None)
    return jax.shard_map(
        per_device, mesh=mesh, in_specs=in_specs, out_specs=out_specs, check_vma=False
    )
```
